32 devices in a mesh: groups: 2 (over x), blk: 16 (over z, y, core).
Axes of the slice: x: 2, y: 2, z: 4, core: 2. Of those that a mesh axis runs over, the one named last changes fastest.
Arguments:
- tokens: bfloat16 [8192, 8192], P(('groups', 'blk')), parts along dimension 0, may hold values from -6 to 6
- shrink_panels: bfloat16 [32, 8192, 64], P(None, 'blk'), may hold values from -0.0625 to 0.0625
- expand_panels: bfloat16 [32, 64, 8192], P(None, None, 'blk'), may hold values from -0.75 to 0.75
- adapter_scale: float32 [32], replicated, may hold values from 0.5 to 2
- block_adapter: int32 [128, 1], P('groups'), parts along dimension 0, may hold values from 0 to 31
- shard_counts: int32 [32], P('groups'), parts along dimension 0, may hold values from 1 to 256, as said below
Outputs:
- update: bfloat16 [8192, 8192], P(('groups', 'blk')), parts along dimension 0
The draws below stay inside these ranges and needn't reach their ends.
There are 2 independent parts, one for each index of `groups`. The reference program is written for one: setup_inputs(seed, part) draws one part's arguments, and reference() takes and returns one part's arrays. A program takes and returns all parts, laid end to end along the dimension named above; an argument that names none is the same for every part. Nothing has to cross between parts.
Inputs may be any that keep to these rules, and one draw needn't show every extreme that they name: `shard_counts`: every shard holds at least one live row; in every draw some shard is full.
All inputs are finite; a program needn't handle non-finite values.
Results may differ from the reference program's by a relative error of at most 0.0049.
Values may be sent and summed in bfloat16 or wider, within the bound.
A program may use at most 128 MiB of HBM per device.

```python
import math
import jax
import jax.numpy as jnp
from jax import lax

D = 8192
R = 64
BLOCK = 64
TOK_DEV = 256
TOKENS = 4096
NBLOCKS = 64
ADAPTERS = 32
N_BLK = 16


def draw_shard_counts(key, part):
    values = jax.random.randint(key, (N_BLK,), 1, TOK_DEV + 1, dtype=jnp.int32)
    full_shard = jax.random.randint(jax.random.fold_in(key, 7), (), 0, N_BLK, dtype=jnp.int32)
    marker = jnp.arange(N_BLK, dtype=jnp.int32) == full_shard
    return jnp.where(marker, TOK_DEV, values).astype(jnp.int32)


def steps_of(key, extent, shards, least, largest):
    factor_of, own = 1.0, jax.random.fold_in(key, 6)
    for position, parts in shards:
        draws = jnp.exp(jax.random.uniform(jax.random.fold_in(own, position), (parts,), jnp.float32, least / len(shards), largest / len(shards)))
        factor_of = factor_of * jnp.repeat(draws, extent[position] // parts).reshape([-1 if axis == position else 1 for axis in range(len(extent))])
    return factor_of


def picks_of(key, rows, number_of, top, lift):
    ranking = jax.random.permutation(jax.random.fold_in(key, 1), number_of)
    favour = ranking
    for power in range(3):
        favour = favour * favour // number_of
    favour = favour * lift // number_of
    tickets = jax.random.randint(jax.random.fold_in(key, 2), (rows, number_of), 0, 4096) + favour
    sure = jax.random.permutation(jax.random.fold_in(key, 3), rows)[jnp.arange(number_of) % rows]
    tickets = jnp.where(jnp.arange(rows)[:, None] == sure[None, :], 1 << 14, tickets)
    score = tickets * number_of + jnp.arange(number_of)
    return lax.top_k(score.astype(jnp.int32), top)[1].astype(jnp.int32)


def scatter_about(own_key, shape, spread, bound, split=(), held_as=jnp.bfloat16):
    gain = steps_of(own_key, shape, split, -0.22, 0.18) if split else 1.0
    result = jax.random.normal(own_key, shape, jnp.float32) * spread * gain
    return jnp.minimum(jnp.maximum(result, -bound), bound).astype(held_as)


def setup_inputs(seed: int = 0, part: int = 0) -> dict:
    seeds = jax.random.split(jax.random.key(seed), 7)
    part_keys = jax.random.split(jax.random.fold_in(seeds[6], part), 7)
    tokens = scatter_about(part_keys[0], (TOKENS, D), 1.0, 6.0, ((0, 16),))
    shrink_panels = scatter_about(seeds[1], (ADAPTERS, D, R), D ** -0.5, 0.0625, ((1, 16),))
    expand_panels = scatter_about(seeds[2], (ADAPTERS, R, D), R ** -0.5, 0.75, ((2, 16),))
    adapter_scale = jnp.clip(jnp.exp(jax.random.uniform(seeds[3], (ADAPTERS,), jnp.float32, math.log(0.5), math.log(2.0))), 0.5, 2.0)
    block_adapter = picks_of(part_keys[4], NBLOCKS, ADAPTERS, 1, 512)
    shard_counts = draw_shard_counts(jax.random.fold_in(jax.random.fold_in(seeds[6], part), 71), part)
    return {"tokens": tokens, "shrink_panels": shrink_panels, "expand_panels": expand_panels, "adapter_scale": adapter_scale, "block_adapter": block_adapter, "shard_counts": shard_counts}


def reference(tokens, shrink_panels, expand_panels, adapter_scale, block_adapter, shard_counts):
    block_count = tokens.shape[0] // BLOCK
    blocked = tokens.reshape(block_count, BLOCK, D)
    adapter_ids = block_adapter[:, 0].astype(jnp.int32)

    def one_block(args):
        block_rows, adapter = args
        down_map = lax.dynamic_index_in_dim(shrink_panels, adapter, 0, keepdims=False)
        up_map = lax.dynamic_index_in_dim(expand_panels, adapter, 0, keepdims=False)
        shrunk = jnp.dot(block_rows, down_map, preferred_element_type=jnp.float32).astype(jnp.bfloat16)
        scale_value = lax.dynamic_index_in_dim(adapter_scale, adapter, 0, keepdims=False)
        return jnp.dot(shrunk, up_map, preferred_element_type=jnp.float32) * scale_value

    expanded = lax.map(one_block, (blocked, adapter_ids)).reshape(TOKENS, D)
    within = jnp.arange(TOK_DEV, dtype=jnp.int32)
    live_rows = (within[None, :] < shard_counts[:, None]).reshape(TOKENS, 1)
    return jnp.where(live_rows, expanded, 0.0).astype(jnp.bfloat16)
```

```python
import functools

import jax
import jax.numpy as jnp
from jax import lax
from jax.experimental import pallas as pl
from jax.experimental.pallas import tpu as pltpu
from jax.sharding import PartitionSpec as P

BLOCK = 64
CHUNKS = 4
MESH = pl.DeviceIdType.MESH


def kernel(
    n, groups,
    ids, scale, counts, tok_h, s_h, e_h, out_h,
    tok, ps, pe, rs, re, gs, ge, ss, se, acc, shr, out_v,
    loc, st_s, st_r, fw_s, fw_r, ax_s, ax_r, osem,
):
    g, me = lax.axis_index("groups"), lax.axis_index("blk")
    h = n // 2
    half, pos = me // h, me % h
    partner = (me + h) % n
    adapters, rank, feats = s_h.shape
    blocks = ss.shape[2]
    share = adapters // groups
    size = share // CHUNKS
    quarter = me // max(n // 4, 1)
    inner = jnp.logical_and(quarter >= 1, quarter <= 2)
    sources, own, other = (s_h, e_h), (ps, pe), (rs, re)
    sends, slots = (gs, ge), (ss, se)

    local = [
        pltpu.make_async_copy(s_h, ps, loc.at[0]),
        pltpu.make_async_copy(e_h, pe, loc.at[1]),
        pltpu.make_async_copy(tok_h, tok, loc.at[2]),
    ]
    for copy in local:
        copy.start()

    barrier = pltpu.get_barrier_semaphore()

    def greet(group, blk):
        pl.semaphore_signal(
            barrier, inc=1, device_id={"groups": group, "blk": blk}, device_id_type=MESH
        )

    greet(g, partner)
    for step in range(1, groups):
        greet((g + step) % groups, me)

    @pl.loop(1, h)
    def _(k):
        greet(g, half * h + (pos + k) % h)

    pl.semaphore_wait(barrier, 1 + (groups - 1) + (h - 1))

    def remote(src, dst, send_sem, recv_sem, group, blk):
        return pltpu.make_async_remote_copy(
            src_ref=src, dst_ref=dst, send_sem=send_sem, recv_sem=recv_sem,
            device_id={"groups": group, "blk": blk}, device_id_type=MESH,
        )

    def part(group, c):
        return pl.ds(group * share + c * size, size)

    def across(p, c):
        return remote(
            sources[p].at[part(g, c)], other[p].at[part(g, c)],
            st_s.at[p, c], st_r.at[p, c], g, partner,
        )

    def forward(p, c, step):
        return remote(
            other[p].at[part(g, c)], other[p].at[part(g, c)],
            fw_s.at[p, c, step - 1], fw_r.at[p, c, step - 1], (g + step) % groups, me,
        )

    def forwarded(p, c, step):
        rows = part((g - step + groups) % groups, c)
        return remote(
            other[p].at[rows], other[p].at[rows],
            fw_s.at[p, c, step - 1], fw_r.at[p, c, step - 1], (g + step) % groups, me,
        )

    def start_across():
        for p in range(2):
            for c in range(CHUNKS):
                across(p, c).start()

    def to_peer(f, p, d):
        return remote(
            sends[p].at[f, d], slots[p].at[f, pos],
            ax_s.at[f, p, d], ax_r.at[f, p, pos], g, half * h + d,
        )

    def from_peer(f, p, s):
        return remote(
            sends[p].at[f, s], slots[p].at[f, s],
            ax_s.at[f, p, s], ax_r.at[f, p, s], g, half * h + s,
        )

    def gather_and_send(f, p, panel):
        @pl.loop(1, h + 1)
        def _(k):
            d = (pos + k) % h
            for b in range(blocks):
                sends[p][f, d, b] = panel[ids[(half * h + d) * blocks + b]]

        @pl.loop(1, h)
        def _(k):
            to_peer(f, p, (pos + k) % h).start()

        for b in range(blocks):
            slots[p][f, pos, b] = sends[p][f, pos, b]

    @pl.when(inner)
    def _():
        start_across()

    for p in range(2):
        local[p].wait()
        gather_and_send(0, p, own[p])

    @pl.when(jnp.logical_not(inner))
    def _():
        start_across()

    for p in range(2):
        for c in range(CHUNKS):
            across(p, c).wait_recv()
            for step in range(1, groups):
                forward(p, c, step).start()
        for c in range(CHUNKS):
            for step in range(1, groups):
                forwarded(p, c, step).wait_recv()
        gather_and_send(1, p, other[p])

    local[2].wait()
    acc[...] = jnp.zeros_like(acc)

    def columns(f, s):
        owner = (half * (1 - f) + (1 - half) * f) * h + s
        return owner, pl.ds(pl.multiple_of(owner * feats, feats), feats)

    def shrink(f, s):
        _, cols = columns(f, s)
        for b in range(blocks):
            acc[b] += lax.dot_general(
                tok[b * BLOCK:(b + 1) * BLOCK, cols], ss[f, s, b],
                (((1,), (1,)), ((), ())), preferred_element_type=jnp.float32,
            )

    for f in range(2):
        shrink(f, pos)

        @pl.loop(1, h)
        def _(k):
            s = (pos - k + h) % h
            from_peer(f, 0, s).wait_recv()
            shrink(f, s)

    shr[...] = acc[...].astype(shr.dtype)
    count = counts[me]
    row = lax.broadcasted_iota(jnp.int32, (BLOCK, feats), 0)

    def put(owner, cols):
        return pltpu.make_async_copy(out_v.at[:, cols], out_h.at[:, cols], osem.at[owner])

    def expand(f, s):
        owner, cols = columns(f, s)
        for b in range(blocks):
            wide = jnp.dot(shr[b], se[f, s, b], preferred_element_type=jnp.float32)
            wide = wide * scale[ids[me * blocks + b]]
            live = row < count - b * BLOCK
            out_v[b * BLOCK:(b + 1) * BLOCK, cols] = jnp.where(live, wide, 0.0).astype(out_v.dtype)
        put(owner, cols).start()

    for f in range(2):
        expand(f, pos)

        @pl.loop(1, h)
        def _(k):
            s = (pos - k + h) % h
            from_peer(f, 1, s).wait_recv()
            expand(f, s)

    for p in range(2):
        for c in range(CHUNKS):
            across(p, c).wait_send()
            for step in range(1, groups):
                forward(p, c, step).wait_send()
        for f in range(2):
            @pl.loop(1, h)
            def _(k):
                to_peer(f, p, (pos + k) % h).wait_send()

    @pl.loop(0, n)
    def _(owner):
        put(owner, pl.ds(pl.multiple_of(owner * feats, feats), feats)).wait()


def body(n, groups, tokens, shrink_panels, expand_panels, adapter_scale, block_adapter, shard_counts):
    rows, width = tokens.shape
    adapters, feats, rank = shrink_panels.shape
    blocks = rows // BLOCK
    h = n // 2
    bf16 = tokens.dtype
    dma = pltpu.SemaphoreType.DMA
    smem = pl.BlockSpec(memory_space=pltpu.SMEM)
    hbm = pl.BlockSpec(memory_space=pl.ANY)
    panel = pltpu.VMEM((adapters, rank, feats), bf16)
    moved = pltpu.VMEM((2, h, blocks, rank, feats), bf16)
    return pl.pallas_call(
        functools.partial(kernel, n, groups),
        out_shape=jax.ShapeDtypeStruct((rows, width), bf16),
        in_specs=[smem, smem, smem, hbm, hbm, hbm],
        out_specs=hbm,
        scratch_shapes=[
            pltpu.VMEM((rows, width), bf16),
            panel, panel, panel, panel,
            moved, moved, moved, moved,
            pltpu.VMEM((blocks, BLOCK, rank), jnp.float32),
            pltpu.VMEM((blocks, BLOCK, rank), bf16),
            pltpu.VMEM((rows, width), bf16),
            dma((3,)),
            dma((2, CHUNKS)), dma((2, CHUNKS)),
            dma((2, CHUNKS, groups - 1)), dma((2, CHUNKS, groups - 1)),
            dma((2, 2, h)), dma((2, 2, h)),
            dma((n,)),
        ],
        compiler_params=pltpu.CompilerParams(
            collective_id=0, has_side_effects=True, vmem_limit_bytes=56 * 1024 * 1024
        ),
    )(
        block_adapter[:, 0], adapter_scale, shard_counts,
        tokens, jnp.swapaxes(shrink_panels, 1, 2), expand_panels,
    )


def solution(mesh):
    return jax.shard_map(
        functools.partial(body, mesh.shape["blk"], mesh.shape["groups"]),
        mesh=mesh,
        in_specs=(
            P(("groups", "blk"), None),
            P(None, "blk", None),
            P(None, None, "blk"),
            P(),
            P("groups", None),
            P("groups"),
        ),
        out_specs=P(("groups", "blk"), None),
        check_vma=False,
    )
```

```python
import functools

import jax
import jax.numpy as jnp
from jax import lax
from jax.experimental import pallas as pl
from jax.experimental.pallas import tpu as pltpu
from jax.sharding import PartitionSpec as P

BLOCK = 64
CHUNKS = 4
MESH = pl.DeviceIdType.MESH


def kernel(
    n, groups,
    ids, scale, counts, tok_h, s_h, e_h, out_h,
    tok, ps, pe, rs0, re0, rs1, re1, gs, ge, fs, fe, ss, se, guest, psum, pgot, acc, shr, out_v,
    loc, st_s, st_r, fw_s, fw_r, ax_s, ax_r, fx_s, tk_s, tk_r, pt_s, pt_r, osem,
):
    g, me = lax.axis_index("groups"), lax.axis_index("blk")
    h, w = n // 2, n // 4
    half, pos, q, u = me // h, me % h, me // w, me % w
    adapters, rank, feats = s_h.shape
    blocks = ss.shape[1]
    share = adapters // groups
    size = share // CHUNKS
    near_inner, near_outer = 1 + half, 3 * half
    far = (2 - half, 3 - 3 * half)
    inside = half * (3 - q) + (1 - half) * q
    inner, outer = inside == 1, inside == 0
    sources, own = (s_h, e_h), (ps, pe)
    others = ((rs0, re0), (rs1, re1))
    sends, far_sends, slots = (gs, ge), (fs, fe), (ss, se)

    local = [
        pltpu.make_async_copy(s_h, ps, loc.at[0]),
        pltpu.make_async_copy(e_h, pe, loc.at[1]),
        pltpu.make_async_copy(tok_h, tok, loc.at[2]),
    ]
    for copy in local:
        copy.start()

    barrier = pltpu.get_barrier_semaphore()

    def greet(group, blk):
        pl.semaphore_signal(
            barrier, inc=1, device_id={"groups": group, "blk": blk}, device_id_type=MESH
        )

    for quarter in far:
        greet(g, quarter * w + u)
    for step in range(1, groups):
        greet((g + step) % groups, me)

    @pl.loop(1, h)
    def _(k):
        greet(g, half * h + (pos + k) % h)

    pl.semaphore_wait(barrier, 2 + (groups - 1) + (h - 1))

    def remote(src, dst, send_sem, recv_sem, group, blk):
        return pltpu.make_async_remote_copy(
            src_ref=src, dst_ref=dst, send_sem=send_sem, recv_sem=recv_sem,
            device_id={"groups": group, "blk": blk}, device_id_type=MESH,
        )

    def part(group, c):
        return pl.ds(group * share + c * size, size)

    def across(j, p, c):
        return remote(
            sources[p].at[part(g, c)], others[j][p].at[part(g, c)],
            st_s.at[p, c], st_r.at[j, p, c], g, far[0] * w + u,
        )

    def forward(j, p, c, step):
        rows = others[j][p].at[part(g, c)]
        sem = (j, p, c, step - 1)
        return remote(rows, rows, fw_s.at[sem], fw_r.at[sem], (g + step) % groups, me)

    def forwarded(j, p, c, step):
        rows = others[j][p].at[part((g - step + groups) % groups, c)]
        sem = (j, p, c, step - 1)
        return remote(rows, rows, fw_s.at[sem], fw_r.at[sem], (g + step) % groups, me)

    def start_across(j):
        for p in range(2):
            for c in range(CHUNKS):
                across(j, p, c).start()

    def to_peer(p, d):
        return remote(
            sends[p].at[d], slots[p].at[me], ax_s.at[p, d], ax_r.at[p, me], g, half * h + d
        )

    def to_far_peer(j, p, d):
        owner = far[j] * w + u
        return remote(
            far_sends[p].at[j, d], slots[p].at[owner],
            fx_s.at[j, p, d], ax_r.at[p, owner], g, half * h + d,
        )

    def from_owner(p, owner):
        return remote(
            slots[p].at[owner], slots[p].at[owner], ax_s.at[p, 0], ax_r.at[p, owner], g, me
        )

    def near_send(p):
        local[p].wait()

        @pl.loop(1, h + 1)
        def _(k):
            d = (pos + k) % h
            for b in range(blocks):
                sends[p][d, b] = own[p][ids[(half * h + d) * blocks + b]]

        @pl.loop(1, h)
        def _(k):
            to_peer(p, (pos + k) % h).start()

        for b in range(blocks):
            slots[p][me, b] = sends[p][pos, b]

    def end_at(k):
        return (near_outer - 2 * half) * w + (u + k) % w

    def side_at(k):
        return (q - 2 * half) * w + (u + k) % w

    def far_send(j, p):
        panel = others[j][p]

        def pick(d):
            for b in range(blocks):
                far_sends[p][j, d, b] = panel[ids[(half * h + d) * blocks + b]]

        if p == 1 or j == 1:
            @pl.loop(0, w)
            def _(k):
                pick(end_at(k))

            @pl.loop(0, w)
            def _(k):
                to_far_peer(j, p, end_at(k)).start()

        @pl.loop(1, w + 1)
        def _(k):
            pick(side_at(k))

        @pl.loop(1, w)
        def _(k):
            to_far_peer(j, p, side_at(k)).start()

        for b in range(blocks):
            slots[p][far[j] * w + u, b] = far_sends[p][j, side_at(0), b]

    def columns(owner):
        return pl.ds(pl.multiple_of(owner * feats, feats), feats)

    def visit(k):
        v = (u + k) % w
        return remote(
            tok_h.at[:, columns(far[0] * w + v)], guest.at[u],
            tk_s.at[v], tk_r.at[u], g, near_inner * w + v,
        )

    def visited(v):
        return remote(guest.at[v], guest.at[v], tk_s.at[v], tk_r.at[v], g, me)

    def back(v):
        return remote(psum.at[v], pgot.at[u], pt_s.at[v], pt_r.at[u], g, near_outer * w + v)

    def came_back(v):
        return remote(pgot.at[v], pgot.at[v], pt_s.at[v], pt_r.at[v], g, me)

    def down(rows, panel):
        return lax.dot_general(
            rows, panel, (((1,), (1,)), ((), ())), preferred_element_type=jnp.float32
        )

    @pl.when(inner)
    def _():
        start_across(0)
        for p in range(2):
            near_send(p)
        for j in range(2):
            for p in range(2):
                for c in range(CHUNKS):
                    across(j, p, c).wait_recv()
                    for step in range(1, groups):
                        forward(j, p, c, step).start()
                for c in range(CHUNKS):
                    for step in range(1, groups):
                        forwarded(j, p, c, step).wait_recv()
                far_send(j, p)
                if j == 0 and p == 0:
                    @pl.loop(0, w)
                    def _(k):
                        v = (u + k) % w
                        visited(v).wait_recv()
                        for b in range(blocks):
                            panel = rs0[ids[(near_outer * w + v) * blocks + b]]
                            rows = guest[v, b * BLOCK:(b + 1) * BLOCK, :]
                            at = (b % 2) * rank
                            psum[v, b // 2, :, at:at + rank] = down(rows, panel)

                    @pl.loop(0, w)
                    def _(k):
                        back((u + k) % w).start()

    @pl.when(outer)
    def _():
        @pl.loop(0, w)
        def _(k):
            visit(k).start()

        near_send(0)
        start_across(1)
        near_send(1)

    local[2].wait()
    acc[...] = jnp.zeros_like(acc)
    order = (
        q,
        inside * far[0] + (1 - inside) * near_inner,
        inside * far[1] + (1 - inside) * far[0],
        inside * near_outer + (1 - inside) * far[1],
    )

    def each(p, turn, use):
        @pl.loop(0, w)
        def _(k):
            owner = order[turn] * w + (u - k + w) % w
            absent = k > 0
            if turn in (1, 2):
                absent = jnp.logical_or(absent, outer)
            if turn == 3:
                absent = k >= 0

            @pl.when(absent)
            def _():
                from_owner(p, owner).wait_recv()

            use(owner)

    def shrink(owner):
        for b in range(blocks):
            acc[b] += down(tok[b * BLOCK:(b + 1) * BLOCK, columns(owner)], ss[owner, b])

    for turn in range(4):
        if turn != 2:
            each(0, turn, shrink)
            continue

        @pl.when(inner)
        def _():
            each(0, 2, shrink)

        @pl.when(outer)
        def _():
            @pl.loop(0, w)
            def _(k):
                v = (u - k + w) % w
                came_back(v).wait_recv()
                for b in range(blocks):
                    at = (b % 2) * rank
                    acc[b] += pgot[v, b // 2, :, at:at + rank]

    shr[...] = acc[...].astype(shr.dtype)
    count = counts[me]
    row = lax.broadcasted_iota(jnp.int32, (BLOCK, feats), 0)

    def put(owner):
        cols = columns(owner)
        return pltpu.make_async_copy(out_v.at[:, cols], out_h.at[:, cols], osem.at[owner])

    def expand(owner):
        for b in range(blocks):
            wide = jnp.dot(shr[b], se[owner, b], preferred_element_type=jnp.float32)
            wide = wide * scale[ids[me * blocks + b]]
            live = row < count - b * BLOCK
            out_v[b * BLOCK:(b + 1) * BLOCK, columns(owner)] = jnp.where(
                live, wide, 0.0
            ).astype(out_v.dtype)
        put(owner).start()

    for turn in range(4):
        each(1, turn, expand)

    for p in range(2):
        for c in range(CHUNKS):
            across(0, p, c).wait_send()

        @pl.loop(1, h)
        def _(k):
            to_peer(p, (pos + k) % h).wait_send()

    @pl.when(inner)
    def _():
        for j in range(2):
            for p in range(2):
                for c in range(CHUNKS):
                    for step in range(1, groups):
                        forward(j, p, c, step).wait_send()

                @pl.loop(1, w)
                def _(k):
                    to_far_peer(j, p, side_at(k)).wait_send()

                if p == 1 or j == 1:
                    @pl.loop(0, w)
                    def _(k):
                        to_far_peer(j, p, end_at(k)).wait_send()

        @pl.loop(0, w)
        def _(k):
            back((u + k) % w).wait_send()

    @pl.when(outer)
    def _():
        @pl.loop(0, w)
        def _(k):
            visit(k).wait_send()

    @pl.loop(0, n)
    def _(owner):
        put(owner).wait()


def body(n, groups, tokens, shrink_panels, expand_panels, adapter_scale, block_adapter, shard_counts):
    rows, width = tokens.shape
    adapters, feats, rank = shrink_panels.shape
    blocks = rows // BLOCK
    h, w = n // 2, n // 4
    bf16 = tokens.dtype
    dma = pltpu.SemaphoreType.DMA
    smem = pl.BlockSpec(memory_space=pltpu.SMEM)
    hbm = pl.BlockSpec(memory_space=pl.ANY)
    panel = pltpu.VMEM((adapters, rank, feats), bf16)
    near = pltpu.VMEM((h, blocks, rank, feats), bf16)
    distant = pltpu.VMEM((2, h, blocks, rank, feats), bf16)
    slot = pltpu.VMEM((n, blocks, rank, feats), bf16)
    sums = pltpu.VMEM((w, (blocks + 1) // 2, BLOCK, 2 * rank), jnp.float32)
    return pl.pallas_call(
        functools.partial(kernel, n, groups),
        out_shape=jax.ShapeDtypeStruct((rows, width), bf16),
        in_specs=[smem, smem, smem, hbm, hbm, hbm],
        out_specs=hbm,
        scratch_shapes=[
            pltpu.VMEM((rows, width), bf16),
            panel, panel, panel, panel, panel, panel,
            near, near, distant, distant, slot, slot,
            pltpu.VMEM((w, rows, feats), bf16),
            sums, sums,
            pltpu.VMEM((blocks, BLOCK, rank), jnp.float32),
            pltpu.VMEM((blocks, BLOCK, rank), bf16),
            pltpu.VMEM((rows, width), bf16),
            dma((3,)),
            dma((2, CHUNKS)), dma((2, 2, CHUNKS)),
            dma((2, 2, CHUNKS, groups - 1)), dma((2, 2, CHUNKS, groups - 1)),
            dma((2, h)), dma((2, n)), dma((2, 2, h)),
            dma((w,)), dma((w,)), dma((w,)), dma((w,)),
            dma((n,)),
        ],
        compiler_params=pltpu.CompilerParams(
            collective_id=0, has_side_effects=True, vmem_limit_bytes=60 * 1024 * 1024
        ),
    )(
        block_adapter[:, 0], adapter_scale, shard_counts,
        tokens, jnp.swapaxes(shrink_panels, 1, 2), expand_panels,
    )


def solution(mesh):
    return jax.shard_map(
        functools.partial(body, mesh.shape["blk"], mesh.shape["groups"]),
        mesh=mesh,
        in_specs=(
            P(("groups", "blk"), None),
            P(None, "blk", None),
            P(None, None, "blk"),
            P(),
            P("groups", None),
            P("groups"),
        ),
        out_specs=P(("groups", "blk"), None),
        check_vma=False,
    )
```

```python
import functools

import jax
import jax.numpy as jnp
from jax import lax
from jax.experimental import pallas as pl
from jax.experimental.pallas import tpu as pltpu
from jax.sharding import PartitionSpec as P

BLOCK = 64
CHUNKS = 2
SLICES = 2
MESH = pl.DeviceIdType.MESH


def kernel(
    n, groups,
    ids, scale, counts, tok_h, s_h, e_h, out_h,
    tok, ps, pe, gs, ge, fs, fe, ss, se, guest, psum, pgot, acc, shr, out_v,
    loc, st_s, st_r, fw_s, fw_r, ax_s, ax_r, fx_s, fx_r, tk_s, tk_r, pt_s, pt_r, osem, *distant,
):
    g, me = lax.axis_index("groups"), lax.axis_index("blk")
    h, w = n // 2, n // 4
    half, pos, q, u = me // h, me % h, me // w, me % w
    adapters, rank, feats = s_h.shape
    blocks = ss.shape[2]
    thick = rank // SLICES
    share = adapters // groups
    size = share // CHUNKS
    near_inner, near_outer = 1 + half, 3 * half
    far = (2 - half, 3 - 3 * half)
    inside = half * (3 - q) + (1 - half) * q
    inner, outer = inside == 1, inside == 0
    sources, own = (s_h, e_h), (ps, pe)
    others = [
        [distant[(2 * j + p) * SLICES:(2 * j + p + 1) * SLICES] for p in range(2)]
        for j in range(2)
    ]
    sends, far_sends, slots = (gs, ge), (fs, fe), (ss, se)

    local = [
        pltpu.make_async_copy(s_h, ps, loc.at[0]),
        pltpu.make_async_copy(e_h, pe, loc.at[1]),
        pltpu.make_async_copy(tok_h, tok, loc.at[2]),
    ]
    for copy in local:
        copy.start()

    barrier = pltpu.get_barrier_semaphore()

    def greet(group, blk):
        pl.semaphore_signal(
            barrier, inc=1, device_id={"groups": group, "blk": blk}, device_id_type=MESH
        )

    for quarter in far:
        greet(g, quarter * w + u)
    for step in range(1, groups):
        greet((g + step) % groups, me)

    @pl.loop(1, h)
    def _(k):
        greet(g, half * h + (pos + k) % h)

    pl.semaphore_wait(barrier, 2 + (groups - 1) + (h - 1))

    def remote(src, dst, send_sem, recv_sem, group, blk):
        return pltpu.make_async_remote_copy(
            src_ref=src, dst_ref=dst, send_sem=send_sem, recv_sem=recv_sem,
            device_id={"groups": group, "blk": blk}, device_id_type=MESH,
        )

    def part(group, c):
        return pl.ds(group * share + c * size, size)

    def ranks(r):
        return pl.ds(r * thick, thick)

    def across(j, p, r, c):
        return remote(
            sources[p].at[part(g, c), ranks(r)], others[j][p][r].at[part(g, c)],
            st_s.at[p, r, c], st_r.at[j, p, r, c], g, far[0] * w + u,
        )

    def forward(j, p, r, c, step):
        rows = others[j][p][r].at[part(g, c)]
        sem = (j, p, r, c, step - 1)
        return remote(rows, rows, fw_s.at[sem], fw_r.at[sem], (g + step) % groups, me)

    def forwarded(j, p, r, c, step):
        rows = others[j][p][r].at[part((g - step + groups) % groups, c)]
        sem = (j, p, r, c, step - 1)
        return remote(rows, rows, fw_s.at[sem], fw_r.at[sem], (g + step) % groups, me)

    def start_across(j, p):
        for r in range(SLICES):
            for c in range(CHUNKS):
                across(j, p, r, c).start()

    def to_peer(p, d):
        return remote(
            sends[p].at[d], slots[p].at[me], ax_s.at[p, d], ax_r.at[p, me], g, half * h + d
        )

    def to_far_peer(j, p, r, d):
        owner = far[j] * w + u
        return remote(
            far_sends[p].at[j, d, r], slots[p].at[owner, r],
            fx_s.at[j, p, r, d], fx_r.at[j, p, r, u], g, half * h + d,
        )

    def from_near(p, owner):
        rows = slots[p].at[owner]
        return remote(rows, rows, ax_s.at[p, 0], ax_r.at[p, owner], g, me)

    def from_far(j, p, r, v):
        rows = slots[p].at[far[j] * w + v, r]
        return remote(rows, rows, fx_s.at[j, p, r, 0], fx_r.at[j, p, r, v], g, me)

    def near_send(p):
        local[p].wait()

        @pl.loop(1, h + 1)
        def _(k):
            d = (pos + k) % h
            for b in range(blocks):
                panel = own[p][ids[(half * h + d) * blocks + b]]
                for r in range(SLICES):
                    sends[p][d, r, b] = panel[r * thick:(r + 1) * thick]

        @pl.loop(1, h)
        def _(k):
            to_peer(p, (pos + k) % h).start()

        slots[p][me] = sends[p][pos]

    def end_at(k):
        return (near_outer - 2 * half) * w + (u + k) % w

    def side_at(k):
        return (q - 2 * half) * w + (u + k) % w

    def far_send(j, p, r):
        panel = others[j][p][r]

        def pick(d):
            for b in range(blocks):
                far_sends[p][j, d, r, b] = panel[ids[(half * h + d) * blocks + b]]

        if p == 1 or j == 1:
            @pl.loop(0, w)
            def _(k):
                pick(end_at(k))

            @pl.loop(0, w)
            def _(k):
                to_far_peer(j, p, r, end_at(k)).start()

        @pl.loop(1, w + 1)
        def _(k):
            pick(side_at(k))

        @pl.loop(1, w)
        def _(k):
            to_far_peer(j, p, r, side_at(k)).start()

        slots[p][far[j] * w + u, r] = far_sends[p][j, side_at(0), r]

    def columns(owner):
        return pl.ds(pl.multiple_of(owner * feats, feats), feats)

    def visit(k):
        v = (u + k) % w
        return remote(
            tok_h.at[:, columns(far[0] * w + v)], guest.at[u],
            tk_s.at[v], tk_r.at[u], g, near_inner * w + v,
        )

    def visited(v):
        return remote(guest.at[v], guest.at[v], tk_s.at[v], tk_r.at[v], g, me)

    def back(v):
        return remote(psum.at[v], pgot.at[u], pt_s.at[v], pt_r.at[u], g, near_outer * w + v)

    def came_back(v):
        return remote(pgot.at[v], pgot.at[v], pt_s.at[v], pt_r.at[v], g, me)

    def down(rows, panel):
        return lax.dot_general(
            rows, panel, (((1,), (1,)), ((), ())), preferred_element_type=jnp.float32
        )

    @pl.when(inner)
    def _():
        for p in range(2):
            start_across(0, p)
        for p in range(2):
            near_send(p)
        for j, p, r in [(j, p, r) for j in range(2) for p in range(2) for r in range(SLICES)]:
            for c in range(CHUNKS):
                across(j, p, r, c).wait_recv()
                for step in range(1, groups):
                    forward(j, p, r, c, step).start()
            for c in range(CHUNKS):
                for step in range(1, groups):
                    forwarded(j, p, r, c, step).wait_recv()
            far_send(j, p, r)
            if (j, p, r) == (0, 0, SLICES - 1):
                @pl.loop(0, w)
                def _(k):
                    v = (u + k) % w
                    visited(v).wait_recv()
                    for b in range(blocks):
                        rows = guest[v, b * BLOCK:(b + 1) * BLOCK, :]
                        for i in range(SLICES):
                            panel = others[0][0][i][ids[(near_outer * w + v) * blocks + b]]
                            at = (b % 2) * rank + i * thick
                            psum[v, b // 2, :, at:at + thick] = down(rows, panel)

                @pl.loop(0, w)
                def _(k):
                    back((u + k) % w).start()

    @pl.when(outer)
    def _():
        @pl.loop(0, w)
        def _(k):
            visit(k).start()

        near_send(0)
        start_across(1, 0)
        start_across(1, 1)
        near_send(1)

    local[2].wait()
    acc[...] = jnp.zeros_like(acc)
    def each(p, quarter, j, k0, use):
        @pl.loop(0, w)
        def _(k):
            v = (u - k + w) % w

            @pl.when(k >= k0)
            def _():
                if j is None:
                    from_near(p, quarter * w + v).wait_recv()
                else:
                    for r in range(SLICES):
                        from_far(j, p, r, v).wait_recv()

            use(quarter * w + v)

    def panel_of(slot, owner, b):
        return jnp.concatenate([slot[owner, r, b] for r in range(SLICES)], axis=0)

    def shrink(owner):
        for b in range(blocks):
            acc[b] += down(tok[b * BLOCK:(b + 1) * BLOCK, columns(owner)], panel_of(ss, owner, b))

    each(0, q, None, 1, shrink)

    @pl.when(inner)
    def _():
        for j in range(2):
            each(0, far[j], j, 1, shrink)
        each(0, near_outer, None, 0, shrink)

    @pl.when(outer)
    def _():
        each(0, near_inner, None, 0, shrink)

        @pl.loop(0, w)
        def _(k):
            v = (u - k + w) % w
            came_back(v).wait_recv()
            for b in range(blocks):
                at = (b % 2) * rank
                acc[b] += pgot[v, b // 2, :, at:at + rank]

        each(0, far[1], 1, 0, shrink)

    shr[...] = acc[...].astype(shr.dtype)
    count = counts[me]
    row = lax.broadcasted_iota(jnp.int32, (BLOCK, feats), 0)

    def put(owner):
        cols = columns(owner)
        return pltpu.make_async_copy(out_v.at[:, cols], out_h.at[:, cols], osem.at[owner])

    def expand(owner):
        for b in range(blocks):
            wide = jnp.dot(shr[b], panel_of(se, owner, b), preferred_element_type=jnp.float32)
            wide = wide * scale[ids[me * blocks + b]]
            live = row < count - b * BLOCK
            out_v[b * BLOCK:(b + 1) * BLOCK, columns(owner)] = jnp.where(
                live, wide, 0.0
            ).astype(out_v.dtype)
        put(owner).start()

    each(1, q, None, 1, expand)

    @pl.when(inner)
    def _():
        for j in range(2):
            each(1, far[j], j, 1, expand)
        each(1, near_outer, None, 0, expand)

    @pl.when(outer)
    def _():
        each(1, near_inner, None, 0, expand)
        for j in range(2):
            each(1, far[j], j, 0, expand)

    for p in range(2):
        for r in range(SLICES):
            for c in range(CHUNKS):
                across(0, p, r, c).wait_send()

        @pl.loop(1, h)
        def _(k):
            to_peer(p, (pos + k) % h).wait_send()

    @pl.when(inner)
    def _():
        for j, p, r in [(j, p, r) for j in range(2) for p in range(2) for r in range(SLICES)]:
            for c in range(CHUNKS):
                for step in range(1, groups):
                    forward(j, p, r, c, step).wait_send()

            @pl.loop(1, w)
            def _(k):
                to_far_peer(j, p, r, side_at(k)).wait_send()

            if p == 1 or j == 1:
                @pl.loop(0, w)
                def _(k):
                    to_far_peer(j, p, r, end_at(k)).wait_send()

        @pl.loop(0, w)
        def _(k):
            back((u + k) % w).wait_send()

    @pl.when(outer)
    def _():
        @pl.loop(0, w)
        def _(k):
            visit(k).wait_send()

    @pl.loop(0, n)
    def _(owner):
        put(owner).wait()


def body(n, groups, tokens, shrink_panels, expand_panels, adapter_scale, block_adapter, shard_counts):
    rows, width = tokens.shape
    adapters, feats, rank = shrink_panels.shape
    blocks = rows // BLOCK
    h, w = n // 2, n // 4
    bf16 = tokens.dtype
    dma = pltpu.SemaphoreType.DMA
    smem = pl.BlockSpec(memory_space=pltpu.SMEM)
    hbm = pl.BlockSpec(memory_space=pl.ANY)
    panel = pltpu.VMEM((adapters, rank, feats), bf16)
    slice_of = pltpu.VMEM((adapters, rank // SLICES, feats), bf16)
    moved = (SLICES, blocks, rank // SLICES, feats)
    near = pltpu.VMEM((h, *moved), bf16)
    distant = pltpu.VMEM((2, h, *moved), bf16)
    slot = pltpu.VMEM((n, *moved), bf16)
    sums = pltpu.VMEM((w, (blocks + 1) // 2, BLOCK, 2 * rank), jnp.float32)
    return pl.pallas_call(
        functools.partial(kernel, n, groups),
        out_shape=jax.ShapeDtypeStruct((rows, width), bf16),
        in_specs=[smem, smem, smem, hbm, hbm, hbm],
        out_specs=hbm,
        scratch_shapes=[
            pltpu.VMEM((rows, width), bf16),
            panel, panel,
            near, near, distant, distant, slot, slot,
            pltpu.VMEM((w, rows, feats), bf16),
            sums, sums,
            pltpu.VMEM((blocks, BLOCK, rank), jnp.float32),
            pltpu.VMEM((blocks, BLOCK, rank), bf16),
            pltpu.VMEM((rows, width), bf16),
            dma((3,)),
            dma((2, SLICES, CHUNKS)), dma((2, 2, SLICES, CHUNKS)),
            dma((2, 2, SLICES, CHUNKS, groups - 1)), dma((2, 2, SLICES, CHUNKS, groups - 1)),
            dma((2, h)), dma((2, n)), dma((2, 2, SLICES, h)), dma((2, 2, SLICES, w)),
            dma((w,)), dma((w,)), dma((w,)), dma((w,)),
            dma((n,)),
            *[slice_of] * (4 * SLICES),
        ],
        compiler_params=pltpu.CompilerParams(
            collective_id=0, has_side_effects=True, vmem_limit_bytes=60 * 1024 * 1024
        ),
    )(
        block_adapter[:, 0], adapter_scale, shard_counts,
        tokens, jnp.swapaxes(shrink_panels, 1, 2), expand_panels,
    )


def solution(mesh):
    return jax.shard_map(
        functools.partial(body, mesh.shape["blk"], mesh.shape["groups"]),
        mesh=mesh,
        in_specs=(
            P(("groups", "blk"), None),
            P(None, "blk", None),
            P(None, None, "blk"),
            P(),
            P("groups", None),
            P("groups"),
        ),
        out_specs=P(("groups", "blk"), None),
        check_vma=False,
    )
```
